32 devices in a mesh: pipe: 2 (over x), dp: 4 (over z), tensor: 4 (over y, core).
Axes of the slice: x: 2, y: 2, z: 4, core: 2. Of those that a mesh axis runs over, the one named last changes fastest.
Arguments:
- section_in: bfloat16 [2, 2048, 2048], P('pipe', 'dp'), may hold values from -60 to 60
- ln_gain: float32 [2, 2, 2048], P('pipe'), may hold values from 0.1 to 1.9
- ln_bias: float32 [2, 2, 2048], P('pipe'), may hold values from -2 to 2
- w_qkv: bfloat16 [2, 2048, 3, 2048], P('pipe', None, None, 'tensor'), may hold values from -6 to 6
- b_qkv: float32 [2, 3, 2048], P('pipe', None, 'tensor'), may hold values from -3 to 3
- w_out: bfloat16 [2, 2048, 2048], P('pipe', 'tensor'), may hold values from -0.5 to 0.5
- w_gate: bfloat16 [2, 2048, 5632], P('pipe', None, 'tensor'), may hold values from -0.125 to 0.125
- w_up: bfloat16 [2, 2048, 5632], P('pipe', None, 'tensor'), may hold values from -0.125 to 0.125
- w_down: bfloat16 [2, 5632, 2048], P('pipe', 'tensor'), may hold values from -0.078125 to 0.078125
Outputs:
- section_out: bfloat16 [2, 2048, 2048], P('pipe', 'dp')
- grad_ln_gain: float32 [2, 2, 2048], P('pipe', None, 'dp')
- grad_ln_bias: float32 [2, 2, 2048], P('pipe', None, 'dp')
- grad_qkv: float32 [2, 2048, 3, 2048], P('pipe', 'dp', None, 'tensor')
- grad_qkv_bias: float32 [2, 3, 32, 64], P('pipe', None, 'tensor', 'dp')
- grad_out: float32 [2, 2048, 2048], P('pipe', 'tensor', 'dp')
- grad_gate: float32 [2, 2048, 5632], P('pipe', 'dp', 'tensor')
- grad_up: float32 [2, 2048, 5632], P('pipe', 'dp', 'tensor')
- grad_down: float32 [2, 5632, 2048], P('pipe', 'tensor', 'dp')
The draws below stay inside these ranges and needn't reach their ends.
All inputs are finite; a program needn't handle non-finite values.
Results may differ from the reference program's by a relative error of at most 0.019.
Values may be sent and summed in bfloat16 or wider, within the bound.
No kernel may reach another device: no remote copies, remote signals or barrier semaphores. Data moves between devices by JAX's collectives and lax.ppermute only.
A program may use at most 320 MiB of HBM per device.

```python
import math
import jax
import jax.numpy as jnp
from jax import lax

D = 2048
H = 32
HD = 64
ROT = 16
FF = 5632
LEN = 256
SEQS = 8
TOKENS = 2048


def draw_section_in(key, part):
    subkeys = jax.random.split(key, 1)
    return jnp.clip(jax.random.normal(subkeys[0], (2, TOKENS, D), jnp.float32), -6.0, 6.0).astype(jnp.bfloat16)


def draw_w_qkv(key, part):
    subkeys = jax.random.split(key, 1)
    return (jnp.clip(jax.random.normal(subkeys[0], (2, D, 3, D), jnp.float32), -6.0, 6.0) / math.sqrt(D)).astype(jnp.bfloat16)


def shard_levels(rng, shape, pieces, smallest, high):
    def one(dim, blocks):
        steps = jax.random.uniform(jax.random.fold_in(jax.random.fold_in(rng, 6), dim), (blocks,), jnp.float32, smallest / len(pieces), high / len(pieces))
        return jnp.repeat(jnp.exp(steps), shape[dim] // blocks).reshape((-1,) + (1,) * (len(shape) - dim - 1))

    factor_of = one(*pieces[0])
    for cut in pieces[1:]:
        factor_of = factor_of * one(*cut)
    return factor_of


def bell_draw(key, dims, scale, bound, shards=(), kind=jnp.bfloat16):
    result = jax.random.normal(key, dims, jnp.float32) * scale
    if len(shards) > 0:
        result = shard_levels(key, dims, shards, -0.22, 0.18) * result
    return jnp.clip(result, min=-bound, max=bound).astype(kind)


def setup_inputs(seed: int = 0) -> dict:
    key_list = jax.random.split(jax.random.key(seed), 10)
    section_in = draw_section_in(jax.random.fold_in(key_list[9], 71), 0)
    ln_gain = jnp.clip(1.0 + 0.18 * jax.random.normal(key_list[1], (2, 2, D), jnp.float32), 0.1, 1.9)
    ln_bias = bell_draw(key_list[2], (2, 2, D), 0.3, 2.0, ((0, 2),), jnp.float32)
    w_qkv = draw_w_qkv(jax.random.fold_in(key_list[9], 71), 0)
    b_qkv = bell_draw(key_list[4], (2, 3, D), 0.5, 3.0, ((0, 2), (2, 4)), jnp.float32)
    w_out = bell_draw(key_list[5], (2, D, D), (D // 16) ** -0.5, 0.5, ((0, 2), (1, 4)))
    w_gate = bell_draw(key_list[6], (2, D, FF), D ** -0.5, 0.125, ((0, 2), (2, 4)))
    w_up = bell_draw(key_list[7], (2, D, FF), D ** -0.5, 0.125, ((0, 2), (2, 4)))
    w_down = bell_draw(key_list[8], (2, FF, D), FF ** -0.5, 0.078125, ((0, 2), (1, 4)))
    return dict(section_in=section_in, ln_gain=ln_gain, ln_bias=ln_bias, w_qkv=w_qkv, b_qkv=b_qkv, w_out=w_out, w_gate=w_gate, w_up=w_up, w_down=w_down)


EPSILON = 1e-05
HIGHEST = lax.Precision.HIGHEST

@jax.custom_vjp
def low(v):
    return lax.optimization_barrier(v.astype(jnp.bfloat16)).astype(jnp.float32)

@jax.custom_vjp
def low_back(v):
    return v

def low_keep(v):
    return (low(v), None)

def low_pass(kept, grad):
    return (grad,)

def back_keep(v):
    return (v, None)

def back_low(kept, grad):
    return (low(grad),)
low.defvjp(low_keep, low_pass)
low_back.defvjp(back_keep, back_low)

def layer_norm(rows_in, gain_row, shift_row):
    row_mean = lax.optimization_barrier(jnp.mean(rows_in, axis=-1, keepdims=True))
    centred = rows_in - row_mean
    inv_scale = lax.rsqrt(lax.optimization_barrier(jnp.mean(centred * centred, axis=-1, keepdims=True)) + EPSILON)
    return centred * inv_scale * gain_row + shift_row

def rotary_tables(length, rot_dims):
    position = jnp.arange(length, dtype=jnp.float32)
    frequency = jnp.exp(-jnp.log(10000.0) * jnp.arange(rot_dims // 2, dtype=jnp.float32) * 2.0 / rot_dims)
    angles = position[:, None] * frequency[None, :]
    return (jnp.cos(angles)[:, None, :], jnp.sin(angles)[:, None, :])

def rotate(vector, cosine, sine_table, rot_dims):
    half_rot = rot_dims // 2
    leading = vector[..., :half_rot]
    trailing = vector[..., half_rot:rot_dims]
    return jnp.concatenate([leading * cosine - trailing * sine_table, trailing * cosine + leading * sine_table, vector[..., rot_dims:]], axis=-1)

def attend(block):
    queries, key_rows, value_rows = block
    raw_scores = jnp.einsum('qhd,khd->hqk', queries, key_rows, precision=HIGHEST)
    scores = low_back(raw_scores * 0.125)
    causal = jnp.arange(LEN)[:, None] >= jnp.arange(LEN)[None, :]
    scores = jnp.where(causal[None], scores, -1e+30)
    probability = low(jax.nn.softmax(scores, axis=-1))
    return jnp.einsum('hqk,khd->qhd', probability, value_rows, precision=HIGHEST)

def decoder_layer(params, rows_in):
    norm_gain, norm_shift, qkv_matrix, qkv_shift, out_matrix, gate_matrix, up_matrix, down_matrix = params
    normed = low(layer_norm(rows_in, norm_gain[0], norm_shift[0]))
    projected = jnp.dot(normed, qkv_matrix.reshape(D, 3 * D), precision=HIGHEST) + qkv_shift.reshape(3 * D)
    projected = low_back(projected).reshape(SEQS, LEN, 3, H, HD)
    cosine, sine_table = rotary_tables(LEN, ROT)
    queries = low(rotate(projected[:, :, 0], cosine, sine_table, ROT))
    key_rows = low(rotate(projected[:, :, 1], cosine, sine_table, ROT))
    value_rows = low(projected[:, :, 2])
    attended = lax.map(jax.checkpoint(attend), (queries, key_rows, value_rows))
    attended = low(low_back(attended.reshape(TOKENS, D)))
    middle = rows_in + low_back(jnp.dot(attended, out_matrix, precision=HIGHEST))
    normed2 = low(layer_norm(middle, norm_gain[1], norm_shift[1]))
    gate_pre = low_back(jnp.dot(normed2, gate_matrix, precision=HIGHEST))
    up_pre = low_back(jnp.dot(normed2, up_matrix, precision=HIGHEST))
    inner_low = low(jax.nn.silu(gate_pre) * up_pre)
    return middle + low_back(jnp.dot(inner_low, down_matrix, precision=HIGHEST))

def reference(section_in, ln_gain, ln_bias, w_qkv, b_qkv, w_out, w_gate, w_up, w_down):
    inputs = section_in[0].astype(jnp.float32)
    cotangent = section_in[1].astype(jnp.float32)
    params = tuple((array.astype(jnp.float32) for array in (ln_gain, ln_bias, w_qkv, b_qkv, w_out, w_gate, w_up, w_down)))

    def two_sections(weights, rows_in):
        leading = tuple((array[0] for array in weights))
        trailing = tuple((array[1] for array in weights))
        middle = low(low_back(decoder_layer(leading, rows_in)))
        return decoder_layer(trailing, middle)
    output, pullback = jax.vjp(two_sections, params, inputs)
    gradients, grad_in = pullback(cotangent)
    section_out = jnp.stack([grad_in, output]).astype(jnp.bfloat16)
    gain_grad, shift_grad, qkv_grad, qkv_shift_grad, out_grad, gate_grad, up_grad, down_grad = gradients
    return (section_out, gain_grad, shift_grad, qkv_grad, qkv_shift_grad.reshape(2, 3, H, HD), out_grad, gate_grad, up_grad, down_grad)
```

```python
import functools
import jax
import jax.numpy as jnp
from jax import lax
from jax.experimental import pallas as pl
from jax.experimental.pallas import tpu as pltpu
from jax.sharding import PartitionSpec as P

HD = 64
ROT = 16
LEN = 256
EPSILON = 1e-05
LOW = jnp.bfloat16
WIDE = jnp.float32
CORES = [(0, 1), (1, 0), (2, 3), (3, 2)]
CHIPS = [(0, 2), (2, 0), (1, 3), (3, 1)]


def dot(a, b, dims):
    return lax.dot_general(a, b, (dims, ((), ())), preferred_element_type=WIDE)


NN = ((1,), (0,))
NT = ((1,), (1,))
TN = ((0,), (0,))


def rotary_tables(width):
    half = ROT // 2
    position = jnp.arange(LEN, dtype=WIDE)
    frequency = jnp.exp(-jnp.log(10000.0) * jnp.arange(half, dtype=WIDE) * 2.0 / ROT)
    angles = position[:, None] * frequency[None, :]
    cosine, sine = jnp.cos(angles), jnp.sin(angles)
    rest = HD - ROT
    cos_head = jnp.concatenate([cosine, cosine, jnp.ones((LEN, rest), WIDE)], axis=1)
    sin_head = jnp.concatenate([-sine, sine, jnp.zeros((LEN, rest), WIDE)], axis=1)
    return jnp.tile(cos_head, (1, width // HD)), jnp.tile(sin_head, (1, width // HD))


def partner(u):
    lane = lax.broadcasted_iota(jnp.int32, u.shape, 1) % HD
    width = u.shape[1]
    return jnp.where(lane < ROT // 2, pltpu.roll(u, width - ROT // 2, 1), pltpu.roll(u, ROT // 2, 1))


def causal_mask():
    rows = lax.broadcasted_iota(jnp.int32, (LEN, LEN), 0)
    cols = lax.broadcasted_iota(jnp.int32, (LEN, LEN), 1)
    return rows >= cols


def attn_forward_kernel(p_ref, cos_ref, sin_ref, qkv_ref, lse_ref, att_ref):
    width = att_ref.shape[1]
    pair = 2 * HD
    causal = causal_mask()
    low_lane = lax.broadcasted_iota(jnp.int32, (LEN, pair), 1) < HD
    cos_t, sin_t = cos_ref[...], sin_ref[...]
    for i in range(width // pair):
        at = i * pair
        rot = []
        for part in range(2):
            u = p_ref[:, part * width + at : part * width + at + pair]
            rot.append((u * cos_t + partner(u) * sin_t).astype(LOW))
        q, k = rot
        v = p_ref[:, 2 * width + at : 2 * width + at + pair].astype(LOW)
        qkv_ref[:, at : at + pair] = q
        qkv_ref[:, width + at : width + at + pair] = k
        qkv_ref[:, 2 * width + at : 2 * width + at + pair] = v
        outs = []
        for h in range(2):
            mine = low_lane if h == 0 else jnp.logical_not(low_lane)
            q_h = jnp.where(mine, q, jnp.zeros_like(q))
            scores = dot(q_h, k, NT) * 0.125
            scores = jnp.where(causal, scores, -1e30)
            top = jnp.max(scores, axis=-1, keepdims=True)
            e = jnp.exp(scores - top)
            total = jnp.sum(e, axis=-1, keepdims=True)
            prob = (e / total).astype(LOW)
            lse_ref[:, 2 * i + h : 2 * i + h + 1] = top + jnp.log(total)
            outs.append(dot(prob, v, NN))
        att_ref[:, at : at + pair] = jnp.where(low_lane, outs[0], outs[1]).astype(LOW)


def attn_backward_kernel(qkv_ref, lse_ref, ga_ref, cos_ref, sin_ref, gp_ref):
    width = ga_ref.shape[1]
    pair = 2 * HD
    causal = causal_mask()
    low_lane = lax.broadcasted_iota(jnp.int32, (LEN, pair), 1) < HD
    cos_t, sin_t = cos_ref[...], sin_ref[...]
    for i in range(width // pair):
        at = i * pair
        q = qkv_ref[:, at : at + pair]
        k = qkv_ref[:, width + at : width + at + pair]
        v = qkv_ref[:, 2 * width + at : 2 * width + at + pair]
        ga = ga_ref[:, at : at + pair]
        gq = gk = gv = None
        for h in range(2):
            mine = low_lane if h == 0 else jnp.logical_not(low_lane)
            zero = jnp.zeros_like(q)
            q_h, k_h, ga_h = (jnp.where(mine, a, zero) for a in (q, k, ga))
            scores = dot(q_h, k, NT) * 0.125
            lse = lse_ref[:, 2 * i + h : 2 * i + h + 1]
            prob = jnp.where(causal, jnp.exp(jnp.where(causal, scores - lse, -1e30)), 0.0)
            gprob = dot(ga_h, v, NT)
            inner = jnp.sum(prob * gprob, axis=-1, keepdims=True)
            gs = (prob * (gprob - inner)).astype(LOW)
            parts = (dot(gs, k_h, NN), dot(gs, q_h, TN), dot(prob.astype(LOW), ga_h, TN))
            gq, gk, gv = parts if gq is None else (gq + parts[0], gk + parts[1], gv + parts[2])
        for part, g in enumerate((gq, gk)):
            g = g * 0.125
            g = g * cos_t - partner(g) * sin_t
            gp_ref[:, part * width + at : part * width + at + pair] = g.astype(LOW)
        gp_ref[:, 2 * width + at : 2 * width + at + pair] = gv.astype(LOW)


def attn_forward(projected, cos_t, sin_t):
    width = projected.shape[1] // 3
    shapes = (
        jax.ShapeDtypeStruct((LEN, 3 * width), LOW),
        jax.ShapeDtypeStruct((LEN, 128), WIDE),
        jax.ShapeDtypeStruct((LEN, width), LOW),
    )
    heads = width // HD
    return pl.pallas_call(
        attn_forward_kernel,
        out_shape=shapes,
        in_specs=[pl.BlockSpec(memory_space=pltpu.VMEM)] * 3,
        out_specs=[pl.BlockSpec(memory_space=pltpu.VMEM)] * 3,
        compiler_params=pltpu.CompilerParams(vmem_limit_bytes=16 << 20),
        cost_estimate=pl.CostEstimate(
            flops=4 * heads * LEN * LEN * 256, bytes_accessed=10 * LEN * width, transcendentals=heads * LEN * LEN
        ),
        name="attn_forward",
    )(projected, cos_t, sin_t)


def attn_backward(qkv, lse, ga, cos_t, sin_t):
    width = ga.shape[1]
    heads = width // HD
    return pl.pallas_call(
        attn_backward_kernel,
        out_shape=jax.ShapeDtypeStruct((LEN, 3 * width), LOW),
        in_specs=[pl.BlockSpec(memory_space=pltpu.VMEM)] * 5,
        out_specs=pl.BlockSpec(memory_space=pltpu.VMEM),
        compiler_params=pltpu.CompilerParams(vmem_limit_bytes=16 << 20),
        cost_estimate=pl.CostEstimate(
            flops=10 * heads * LEN * LEN * 256, bytes_accessed=14 * LEN * width, transcendentals=heads * LEN * LEN
        ),
        name="attn_backward",
    )(qkv, lse, ga, cos_t, sin_t)


def standardize(v):
    centred = v - jnp.mean(v, axis=-1, keepdims=True)
    scale = lax.rsqrt(jnp.mean(centred * centred, axis=-1, keepdims=True) + EPSILON)
    return centred * scale, scale


def norm_back(g, v, gain):
    vhat, scale = standardize(v)
    t = g * gain
    back = scale * (
        t - jnp.mean(t, axis=-1, keepdims=True) - vhat * jnp.mean(t * vhat, axis=-1, keepdims=True)
    )
    return back, jnp.sum(g * vhat, axis=0), jnp.sum(g, axis=0)


def body(section_in, ln_gain, ln_bias, w_qkv, b_qkv, w_out, w_gate, w_up, w_down):
    is_first = lax.axis_index("pipe") == 0
    core = lax.axis_index("tensor") % 2
    rows = section_in.shape[1]
    D = section_in.shape[2]
    width = w_out.shape[1]
    FF = w_gate.shape[2]
    seqs = rows // LEN
    half = LEN // 2
    gains, shifts = ln_gain[0], ln_bias[0]
    wqkv = w_qkv[0].reshape(D, 3 * width)
    bqkv = b_qkv[0].reshape(1, 3 * width)
    wout, wgate, wup, wdown = w_out[0], w_gate[0], w_up[0], w_down[0]
    cos_t, sin_t = rotary_tables(2 * HD)

    def my_half(a):
        return lax.dynamic_slice_in_dim(a, core * half, half, 0)

    def other_half(a):
        return lax.dynamic_slice_in_dim(a, (1 - core) * half, half, 0)

    def join(mine):
        other = lax.ppermute(mine, "tensor", CORES)
        return jnp.concatenate(
            [jnp.where(core == 0, mine, other), jnp.where(core == 0, other, mine)], axis=0
        )

    def tensor_sum(partial):
        got = lax.ppermute(other_half(partial), "tensor", CORES)
        chip = (my_half(partial).astype(WIDE) + got.astype(WIDE)).astype(LOW)
        far = lax.ppermute(chip, "tensor", CHIPS)
        return chip.astype(WIDE) + far.astype(WIDE)

    def norm(v, j):
        return (standardize(v)[0] * gains[j] + shifts[j]).astype(LOW)

    def layer_forward(x_half):
        normed = join(norm(x_half, 0))
        projected = dot(normed, wqkv, NN) + bqkv
        qkv, lse, attended = attn_forward(projected, cos_t, sin_t)
        mid = x_half + tensor_sum(dot(attended, wout, NN).astype(LOW))
        normed2 = join(norm(mid, 1))
        gate = dot(normed2, wgate, NN)
        up = dot(normed2, wup, NN)
        inner = (jax.nn.silu(gate) * up).astype(LOW)
        out = mid + tensor_sum(dot(inner, wdown, NN).astype(LOW))
        return out, (x_half, normed, qkv, lse, attended, mid, normed2, gate, up, inner)

    def layer_backward(dy_half, dy_low, kept):
        x_half, normed, qkv, lse, attended, mid, normed2, gate, up, inner = kept
        g_inner = dot(dy_low, wdown, NT)
        sg = jax.nn.sigmoid(gate)
        g_up = (g_inner * gate * sg).astype(LOW)
        g_gate = (g_inner * up * sg * (1.0 + gate * (1.0 - sg))).astype(LOW)
        g_normed2 = tensor_sum((dot(g_gate, wgate, NT) + dot(g_up, wup, NT)).astype(LOW))
        back, gain1, shift1 = norm_back(g_normed2, mid, gains[1])
        g_mid = dy_half + back
        g_mid_low = join(g_mid.astype(LOW))
        g_att = dot(g_mid_low, wout, NT).astype(LOW)
        g_proj = attn_backward(qkv, lse, g_att, cos_t, sin_t)
        g_normed = tensor_sum(dot(g_proj, wqkv, NT).astype(LOW))
        back, gain0, shift0 = norm_back(g_normed, x_half, gains[0])
        grads = (g_up, g_gate, g_mid_low, g_proj, jnp.stack([gain0, gain1, shift0, shift1]))
        return g_mid + back, grads

    own = [section_in[0, s * LEN : (s + 1) * LEN] for s in range(seqs)]
    own_half = [my_half(a).astype(WIDE) for a in own]

    outs = [layer_forward(a)[0] for a in own_half]
    got = [lax.ppermute(a.astype(LOW), "pipe", [(0, 1)]) for a in outs]
    ins = [jnp.where(is_first, a, g.astype(WIDE)) for a, g in zip(own_half, got)]
    results, kept = zip(*[layer_forward(a) for a in ins])
    backs = [layer_backward(a, o, k)[0] for a, o, k in zip(own_half, own, kept)]
    got = [lax.ppermute(a.astype(LOW), "pipe", [(1, 0)]) for a in backs]
    dy_half = [jnp.where(is_first, g, a.astype(LOW)) for a, g in zip(own_half, got)]
    dy_low = [join(a) for a in dy_half]
    backs, grads = zip(*[layer_backward(h.astype(WIDE), a, k) for h, a, k in zip(dy_half, dy_low, kept)])

    section_out = jnp.concatenate(
        [join(jnp.where(is_first, b, r).astype(LOW)) for b, r in zip(backs, results)], axis=0
    )[None]

    def whole(parts):
        return jnp.concatenate(parts, axis=0)

    normed, attended, normed2, inner = (whole([k[i] for k in kept]) for i in (1, 4, 6, 9))
    g_up, g_gate, g_mid_low, g_proj = (whole([g[i] for g in grads]) for i in range(4))
    dy = whole(dy_low)
    small = sum(g[4] for g in grads)
    small = small + lax.ppermute(small, "tensor", CORES)

    def scatter(a, dim):
        return lax.psum_scatter(a, "dp", scatter_dimension=dim, tiled=True)

    down_sum = scatter(dot(inner, dy, TN).astype(LOW), 1).astype(WIDE)[None]
    gate_sum = scatter(dot(normed2, g_gate, TN).astype(LOW), 0).astype(WIDE)[None]
    up_sum = scatter(dot(normed2, g_up, TN).astype(LOW), 0).astype(WIDE)[None]
    out_sum = scatter(dot(attended, g_mid_low, TN).astype(LOW), 1).astype(WIDE)[None]
    qkv_sum = scatter(dot(normed, g_proj, TN).astype(LOW), 0).astype(WIDE).reshape(1, -1, 3, width)
    small = scatter(small, 1)
    bias = jnp.sum(g_proj.astype(WIDE), axis=0).reshape(3, width // HD, HD)
    bias = scatter(bias, 2)[None]
    return (
        section_out,
        small[None, :2],
        small[None, 2:],
        qkv_sum,
        bias,
        out_sum,
        gate_sum,
        up_sum,
        down_sum,
    )


def solution(mesh):
    return jax.shard_map(
        body,
        mesh=mesh,
        in_specs=(
            P("pipe", "dp", None),
            P("pipe", None, None),
            P("pipe", None, None),
            P("pipe", None, None, "tensor"),
            P("pipe", None, "tensor"),
            P("pipe", "tensor", None),
            P("pipe", None, "tensor"),
            P("pipe", None, "tensor"),
            P("pipe", "tensor", None),
        ),
        out_specs=(
            P("pipe", "dp", None),
            P("pipe", None, "dp"),
            P("pipe", None, "dp"),
            P("pipe", "dp", None, "tensor"),
            P("pipe", None, "tensor", "dp"),
            P("pipe", "tensor", "dp"),
            P("pipe", "dp", "tensor"),
            P("pipe", "dp", "tensor"),
            P("pipe", "tensor", "dp"),
        ),
        check_vma=False,
    )
```
